32 devices in a mesh: gx: 4 (over z), gy: 4 (over y, core), gz: 2 (over x).
Axes of the slice: x: 2, y: 2, z: 4, core: 2. Of those that a mesh axis runs over, the one named last changes fastest.
Arguments:
- solution: float32 [64, 64, 256], P('gx', 'gy', 'gz'), may hold values from -6 to 6
- right_side: float32 [64, 64, 256], P('gx', 'gy', 'gz'), may hold values from -6 to 6
Outputs:
- improved: float32 [64, 64, 256], P('gx', 'gy', 'gz')
The draws below stay inside these ranges and needn't reach their ends.
All inputs are finite; a program needn't handle non-finite values.
Results may differ from the reference program's by a relative error of at most 0.00015.
Values sent between devices are 32-bit elements; how exact they have to be, the bound alone decides.
A program may use at most 64 MiB of HBM per device.

```python
import jax
import jax.numpy as jnp
from jax import lax

LEVELS = 3
DEGREE = 2
SWEEPS = 2
NX = 64
NY = 64
NZ = 256


def levels(stream_key, shape, shards, low, largest):
    loudness = 1.0
    for dim, parts in shards:
        draws = jax.random.uniform(jax.random.fold_in(jax.random.fold_in(stream_key, 6), dim), (parts,), jnp.float32, low / len(shards), largest / len(shards))
        loudness = loudness * jnp.repeat(jnp.exp(draws), shape[dim] // parts).reshape((-1,) + (1,) * (len(shape) - 1 - dim))
    return loudness


def normal_values(key, shape, scale, most, shards=(), kind=jnp.bfloat16):
    result = scale * jax.random.normal(key, shape, jnp.float32)
    if shards:
        result = result * levels(key, shape, shards, -0.22, 0.18)
    return jnp.clip(result, -most, most).astype(kind)


def setup_inputs(seed: int = 0) -> dict:
    key_list = jax.random.split(jax.random.key(seed), 3)
    solution = normal_values(key_list[0], (NX, NY, NZ), 1.0, 6.0, ((0, 4), (1, 4), (2, 2)), jnp.float32)
    right_side = normal_values(key_list[1], (NX, NY, NZ), 1.0, 6.0, ((0, 4), (1, 4), (2, 2)), jnp.float32)
    return {"solution": solution, "right_side": right_side}


stiff_matrix = ((7.0 / 3.0, -8.0 / 3.0, 1.0 / 3.0), (-8.0 / 3.0, 16.0 / 3.0, -8.0 / 3.0), (1.0 / 3.0, -8.0 / 3.0, 7.0 / 3.0))
mass_matrix = ((4.0 / 30.0, 2.0 / 30.0, -1.0 / 30.0), (2.0 / 30.0, 16.0 / 30.0, 2.0 / 30.0), (-1.0 / 30.0, 2.0 / 30.0, 4.0 / 30.0))
cheb_centre = 1.32
cheb_half = 1.1
cheb_sigma = 1.2


def along_axis(values, dim_index, matrix):
    inner_len = values.shape[dim_index] - 4
    parity = jnp.arange(inner_len) % 2 == 0
    vertex = (matrix[2][0], matrix[2][1], matrix[2][2] + matrix[0][0], matrix[0][1], matrix[0][2])
    middle = (0.0, matrix[1][0], matrix[1][1], matrix[1][2], 0.0)
    shape_list = [1, 1, 1]
    shape_list[dim_index] = inner_len
    summed = None
    for offset in range(5):
        weight = jnp.where(parity, vertex[offset], middle[offset]).astype(jnp.float32).reshape(shape_list)
        shifted = lax.slice_in_dim(values, offset, offset + inner_len, 1, dim_index)
        summed = weight * shifted if offset == 0 else summed + weight * shifted
    return summed


def apply_operator(padded, level_num):
    mass_z = along_axis(padded, 2, mass_matrix)
    stiff_z = along_axis(padded, 2, stiff_matrix)
    mass_yz = along_axis(mass_z, 1, mass_matrix)
    stiff_y = along_axis(mass_z, 1, stiff_matrix)
    stiff_only_z = along_axis(stiff_z, 1, mass_matrix)
    return (2.0 ** level_num) * (along_axis(mass_yz, 0, stiff_matrix) + along_axis(stiff_y + stiff_only_z, 0, mass_matrix))


def inverse_diagonal(new_shape, level_num):
    stiff_list = []
    mass_list = []
    for dim_index in range(3):
        even_node = jnp.arange(new_shape[dim_index]) % 2 == 0
        shape_list = [1, 1, 1]
        shape_list[dim_index] = new_shape[dim_index]
        stiff_list.append(jnp.where(even_node, 14.0 / 3.0, 16.0 / 3.0).astype(jnp.float32).reshape(shape_list))
        mass_list.append(jnp.where(even_node, 8.0 / 30.0, 16.0 / 30.0).astype(jnp.float32).reshape(shape_list))
    stiff_first, stiff_second, stiff_third = stiff_list
    mass_first, mass_second, mass_third = mass_list
    diagonal = (2.0 ** level_num) * (stiff_first * mass_second * mass_third + mass_first * stiff_second * mass_third + mass_first * mass_second * stiff_third)
    return 1.0 / diagonal


def along_dim_product(matrix, values, dim_index):
    einsum_forms = ("ap,pyz->ayz", "ap,xpz->xaz", "ap,xyp->xya")
    return jnp.einsum(einsum_forms[dim_index], matrix, values, precision=lax.Precision.HIGHEST)


def prolong_matrix(fine_count, coarse_len):
    row_index = jnp.arange(fine_count + 4)[:, None]
    col_index = jnp.arange(coarse_len)[None, :]
    half_index = row_index // 2
    offset = col_index - half_index
    even_row = row_index % 2 == 0
    even_half = half_index % 2 == 0
    odd_even = jnp.where(offset == 0, -0.125, jnp.where(offset == 1, 0.75, jnp.where(offset == 2, 0.375, 0.0)))
    odd_odd = jnp.where(offset == 1, 0.375, jnp.where(offset == 2, 0.75, jnp.where(offset == 3, -0.125, 0.0)))
    vertex = jnp.where(offset == 1, 1.0, 0.0)
    entries = jnp.where(even_row, vertex, jnp.where(even_half, odd_even, odd_odd))
    entries = jnp.where(row_index == fine_count + 3, 0.0, entries)
    return entries.astype(jnp.float32)


def restrict_matrix(coarse_count, length):
    row_index = jnp.arange(coarse_count)[:, None]
    col_index = jnp.arange(length)[None, :]
    offset = col_index - 2 * row_index
    even_row = row_index % 2 == 0
    outer = jnp.where(even_row, -0.125, 0.0)
    inner = jnp.where(even_row, 0.375, 0.75)
    entries = jnp.where(offset == 3, 1.0, jnp.where((offset == 0) | (offset == 6), outer, jnp.where((offset == 2) | (offset == 4), inner, 0.0)))
    return entries.astype(jnp.float32)


def prolongate(values, fine_shape):
    for dim_index in range(3):
        matrix = prolong_matrix(fine_shape[dim_index], values.shape[dim_index])
        values = along_dim_product(matrix, values, dim_index)
    return values


def restrict_residual(values, coarse_shape):
    for dim_index in range(3):
        matrix = restrict_matrix(coarse_shape[dim_index], values.shape[dim_index])
        values = along_dim_product(matrix, values, dim_index)
    return values


def operator_full(values, level_num):
    return apply_operator(jnp.pad(values, 2), level_num)


def chebyshev_full(level_num, solution, residual, sweep_count):
    inverse = inverse_diagonal(residual.shape, level_num)
    direction = (inverse * residual) * (1.0 / cheb_centre)
    solution = solution + direction
    ratio = 1.0 / cheb_sigma
    for sweep_step in range(1, sweep_count):
        residual = residual - operator_full(direction, level_num)
        ratio_next = 1.0 / (2.0 * cheb_sigma - ratio)
        direction = (ratio_next * ratio) * direction + (2.0 * ratio_next / cheb_half) * (inverse * residual)
        solution = solution + direction
        ratio = ratio_next
    return solution, residual, direction


def vcycle_full(level_num, solution, residual):
    if level_num == LEVELS - 1:
        solution, residual, direction = chebyshev_full(level_num, solution, residual, SWEEPS)
        return solution
    solution, residual, direction = chebyshev_full(level_num, solution, residual, DEGREE)
    residual = residual - operator_full(direction, level_num)
    coarse_shape = tuple(extent // 2 for extent in residual.shape)
    coarse_rhs = restrict_residual(jnp.pad(residual, 3), coarse_shape)
    coarse_sol = vcycle_full(level_num + 1, jnp.zeros(coarse_shape, jnp.float32), coarse_rhs)
    correction = prolongate(jnp.pad(coarse_sol, 2), residual.shape)[2:-2, 2:-2, 2:-2]
    solution = solution + correction
    residual = residual - operator_full(correction, level_num)
    solution, residual, direction = chebyshev_full(level_num, solution, residual, DEGREE)
    return solution


def reference(solution, right_side):
    residual = right_side - operator_full(solution, 0)
    return vcycle_full(0, solution, residual)
```

```python
import functools

import jax
import jax.numpy as jnp
import numpy as np
from jax import lax
from jax.experimental import pallas as pl
from jax.experimental.pallas import tpu as pltpu
from jax.sharding import PartitionSpec as P

F32 = jnp.float32
BF16 = jnp.bfloat16
MESH = pl.DeviceIdType.MESH
H = 8
ZR = 32
REACH = 3

RHO0 = 1.0 / 1.2
RHO1 = 1.0 / (2.4 - RHO0)
FIRST = 1.0 / 1.32
KEEP = RHO1 * RHO0
STEP = 2.0 * RHO1 / 1.1


def band_matrices(size, cyclic):
    mass = np.zeros((size, size), np.float32)
    stiff = np.zeros((size, size), np.float32)
    for out in range(size):
        if out % 2 == 0:
            taps = ((-2, -1, 1), (-1, 2, -8), (0, 8, 14), (1, 2, -8), (2, -1, 1))
        else:
            taps = ((-1, 2, -8), (0, 16, 16), (1, 2, -8))
        for off, m, k in taps:
            src = out + off
            if cyclic:
                src %= size
            if 0 <= src < size:
                mass[src, out] += m
                stiff[src, out] += k
    return np.concatenate([mass, stiff], axis=1)


def restrict_taps(g):
    if g % 2 == 0:
        return ((-3, -0.125), (-1, 0.375), (0, 1.0), (1, 0.375), (3, -0.125))
    return ((-1, 0.75), (0, 1.0), (1, 0.75))


def prolong_taps(f):
    if f % 2 == 0:
        return ((f // 2, 1.0),)
    q = f // 4
    if f % 4 == 1:
        return ((2 * q, 0.375), (2 * q + 1, 0.75), (2 * q + 2, -0.125))
    return ((2 * q, -0.125), (2 * q + 1, 0.75), (2 * q + 2, 0.375))


def transfer(taps, outs, out_pos, in_pos, n_out, n_in, scale):
    m = np.zeros((n_out, n_in), np.float32)
    for o in outs:
        for s, w in taps(o):
            row, col = out_pos(o), in_pos(scale * o + s if scale else s)
            if col is not None and 0 <= col < n_in:
                m[row, col] += w
    return m


def zdot(v, w):
    hi = v.astype(BF16)
    lo = (v - hi.astype(F32)).astype(BF16)
    return jnp.dot(hi, w, preferred_element_type=F32) + jnp.dot(
        lo, w, preferred_element_type=F32
    )


def exact(a, b):
    return jnp.dot(a, b, preferred_element_type=F32, precision=lax.Precision.HIGHEST)


def y_filters(mz, kz):
    rows = mz.shape[0]
    even = lax.broadcasted_iota(jnp.int32, mz.shape, 0) % 2 == 0

    def sums(v):
        s1 = pltpu.roll(v, 1, 0) + pltpu.roll(v, rows - 1, 0)
        s2 = pltpu.roll(v, 2, 0) + pltpu.roll(v, rows - 2, 0)
        return s1, jnp.where(even, s2, 0.0)

    m1, m2 = sums(mz)
    k1, k2 = sums(kz)
    md = jnp.where(even, 8.0, 16.0)
    kd = jnp.where(even, 14.0, 16.0)
    first = md * mz + 2.0 * m1 - m2
    second = (kd * mz - 8.0 * m1 + m2) + (md * kz + 2.0 * k1 - k2)
    return first, second


def kernel(
    geo, u_ref, b_ref, w0, w1, w2, rz0, ry0, rz1, ry1, pz1, py1, pz0, py0, out_ref,
    ue, be, d0, r0, a0, c0, packs, unpacks, blk, zin, g1, d1, r1, s1, a1, c1,
    r2, d2, a2, t2, send, recv, zsend, zrecv, gsend, grecv, gzsend, gzrecv,
):
    nx, ny, nz, bx, by, bz, wx, wy = geo
    ix, iy, iz = lax.axis_index("gx"), lax.axis_index("gy"), lax.axis_index("gz")
    full_x, full_y = wx == nx, wy == ny
    cx, cy, cz = bx // 2, by // 2, bz // 2
    start_x = 0 if full_x else ix - REACH
    start_y = 0 if full_y else iy - REACH

    def at(axis, off):
        return (
            ix + off if axis == 0 else ix,
            iy + off if axis == 1 else iy,
            iz + off if axis == 2 else iz,
        )

    place = (ix, iy, iz)
    counts = (nx, ny, nz)

    def there(axis, off):
        pos = place[axis] + off
        return (pos >= 0) & (pos < counts[axis])

    spans = (wx - 1 if full_x else REACH, wy - 1 if full_y else REACH, 1 if nz > 1 else 0)
    offsets = [[o for o in range(-s, s + 1) if o] for s in spans]

    ue[...] = jnp.zeros_like(ue)
    be[...] = jnp.zeros_like(be)
    unpacks[...] = jnp.zeros_like(unpacks)
    zin[...] = jnp.zeros_like(zin)
    g1[...] = jnp.zeros_like(g1)
    ue[H : H + bx, H : H + by, :bz] = u_ref[...]
    be[H : H + bx, H : H + by, :bz] = b_ref[...]

    barrier = pltpu.get_barrier_semaphore()
    total = 0
    for axis in range(3):
        for off in offsets[axis]:
            ok = there(axis, off)
            total = total + ok.astype(jnp.int32)

            @pl.when(ok)
            def _():
                pl.semaphore_signal(
                    barrier, inc=1, device_id=at(axis, off), device_id_type=MESH
                )

    pl.semaphore_wait(barrier, total)

    def remote(src, dst, ss, rs, axis, off):
        return pltpu.make_async_remote_copy(
            src_ref=src, dst_ref=dst, send_sem=ss, recv_sem=rs,
            device_id=at(axis, off), device_id_type=MESH,
        )

    def start_if(axis, off, copies):
        @pl.when(there(axis, off))
        def _():
            for c in copies:
                c.start()

    def recv_if(axis, off, copies):
        @pl.when(there(axis, -off))
        def _():
            for c in copies:
                c.wait_recv()

    def sent_if(axis, off, copies):
        @pl.when(there(axis, off))
        def _():
            for c in copies:
                c.wait_send()

    L = bz

    def x_copies(off):
        res = []
        for n, (ref, ext, w) in enumerate(((u_ref, ue, H), (b_ref, be, H - 2))):
            k = n * 2 + (off > 0)
            lo = bx - w if off > 0 else 0
            dst = H - w if off > 0 else H + bx
            res.append(
                remote(
                    ref.at[lo : lo + w],
                    ext.at[dst : dst + w, H : H + by, :L],
                    send.at[k], recv.at[k], 0, off,
                )
            )
        return res

    def y_copies(off):
        res = []
        for n, (ref, ext) in enumerate(((u_ref, ue), (b_ref, be))):
            k = 4 + n * 2 + (off > 0)
            lo = by - H if off > 0 else 0
            dst = 0 if off > 0 else H + by
            res.append(
                remote(
                    ref.at[:, lo : lo + H],
                    ext.at[H : H + bx, dst : dst + H, :L],
                    send.at[k], recv.at[k], 1, off,
                )
            )
        return res

    def corner_copies(off):
        res = []
        for n, (ext, w) in enumerate(((ue, H), (be, H - 2))):
            for side in range(2):
                k = 8 + n * 4 + side * 2 + (off > 0)
                xs = H - w if side == 0 else H + bx
                lo = by if off > 0 else H
                dst = 0 if off > 0 else H + by
                res.append(
                    remote(
                        ext.at[xs : xs + w, lo : lo + H, :L],
                        ext.at[xs : xs + w, dst : dst + H, :L],
                        send.at[k], recv.at[k], 1, off,
                    )
                )
        return res

    both = (-1, 1)
    for off in both:
        start_if(0, off, x_copies(off))
    for off in both:
        start_if(1, off, y_copies(off))
    for off in both:
        recv_if(0, off, x_copies(off))
    for off in both:
        start_if(1, off, corner_copies(off))
    for off in both:
        recv_if(1, off, y_copies(off) + corner_copies(off))

    per = L // H
    lane = lax.broadcasted_iota(jnp.int32, (by + 2 * H, L), 1)
    groups = (bx + 2 * H) // per
    if nz > 1:
        for n, ext in enumerate((ue, be)):
            for g in range(groups):
                low = jnp.zeros((by + 2 * H, L), F32)
                high = jnp.zeros((by + 2 * H, L), F32)
                for k in range(per):
                    plane = ext[g * per + k, :, :L]
                    here = (lane // H) == k
                    low = jnp.where(here, pltpu.roll(plane, (k * H) % L, 1), low)
                    high = jnp.where(here, pltpu.roll(plane, ((k + 1) * H) % L, 1), high)
                packs[0, n, g] = low
                packs[1, n, g] = high

        def z_copies(off):
            k = int(off > 0)
            return [remote(packs.at[k], unpacks.at[k], zsend.at[k], zrecv.at[k], 2, off)]

        for off in both:
            start_if(2, off, z_copies(off))
        for off in both:
            recv_if(2, off, z_copies(off))
        for n, ext in enumerate((ue, be)):
            for g in range(groups):
                upper, lower = unpacks[0, n, g], unpacks[1, n, g]
                for k in range(per):
                    up = pltpu.roll(upper, (L - k * H) % L, 1)
                    lo = pltpu.roll(lower, (L - (k + 1) * H) % L, 1)
                    ext[g * per + k, :, L:] = jnp.where(
                        lane < H, up, jnp.where(lane >= L - H, lo, 0.0)
                    )

    def masks_and_diagonals(level, rows, lanes, y_first, y_end, z_of_lane, z_ok, z_first):
        yy = lax.broadcasted_iota(jnp.int32, (rows, lanes), 0)
        zz = lax.broadcasted_iota(jnp.int32, (rows, lanes), 1)
        y_even, z_even = yy % 2 == 0, zz % 2 == 0
        gy = y_first + yy
        gz = z_first + z_of_lane(zz)
        n_y, n_z = (ny * by) >> level, (nz * bz) >> level
        ok = (gy >= 0) & (gy < n_y) & (yy < y_end) & (gz >= 0) & (gz < n_z) & z_ok(zz)
        mask = jnp.where(ok, 1.0, 0.0)
        my = jnp.where(y_even, 8.0, 16.0) / 30.0
        mz = jnp.where(z_even, 8.0, 16.0) / 30.0
        ky = jnp.where(y_even, 14.0, 16.0) / 3.0
        kz = jnp.where(z_even, 14.0, 16.0) / 3.0
        inv = []
        for kx, mx in ((14.0 / 3.0, 8.0 / 30.0), (16.0 / 3.0, 16.0 / 30.0)):
            diag = 2.0**level * (kx * my * mz + mx * ky * mz + mx * my * kz)
            inv.append(mask / diag)
        return mask, inv

    def filter_planes(src, w, acc, first, pairs, rows, lanes):
        def body(p, carry):
            x = first + 2 * p
            v = src[pl.ds(x, 2)].reshape(2 * rows, lanes)
            prod = zdot(v, w[...])
            for k in range(2):
                part = prod[k * rows : (k + 1) * rows]
                a, c = y_filters(part[:, :lanes], part[:, lanes:])
                acc[0, x + k] = a
                acc[1, x + k] = c
            return carry

        lax.fori_loop(0, pairs, body, 0)

    def applied(acc, first, pairs, level, use):
        scale = 2.0**level / 2700.0

        def body(p, carry):
            x = first + 2 * p
            a = [acc[0, x + k] for k in range(-2, 4)]
            c = [acc[1, x + k] for k in range(-2, 4)]
            even = (14.0 * a[2] - 8.0 * (a[1] + a[3]) + (a[0] + a[4])) + (
                8.0 * c[2] + 2.0 * (c[1] + c[3]) - (c[0] + c[4])
            )
            odd = (16.0 * a[3] - 8.0 * (a[2] + a[4])) + (16.0 * c[3] + 2.0 * (c[2] + c[4]))
            use(x, 0, scale * even)
            use(x + 1, 1, scale * odd)
            return carry

        lax.fori_loop(0, pairs, body, 0)

    rows0, lanes0 = by + 2 * H, 2 * bz
    mask0, inv0 = masks_and_diagonals(
        0, rows0, lanes0, iy * by - H, rows0,
        lambda z: jnp.where(z < bz + bz // 2, z, z - 2 * bz), lambda z: z >= 0, iz * bz,
    )

    def x_mask(level, x, x_first):
        g = x_first + x
        return jnp.where((g >= 0) & (g < ((nx * bx) >> level)), 1.0, 0.0).astype(F32)

    gx0 = ix * bx - H

    def use_residual(x, odd, av):
        r = be[x] - av
        r0[x] = r
        d0[x] = (inv0[odd] * (FIRST * x_mask(0, x, gx0))) * r

    filter_planes(ue, w0, a0, 0, (bx + 16) // 2, rows0, lanes0)
    applied(a0, 2, (bx + 12) // 2, 0, use_residual)
    own0 = (slice(H, H + bx), slice(H, H + by), slice(0, bz))
    out_ref[...] = u_ref[...] + d0[own0]

    def use_step(x, odd, av):
        r = r0[x] - av
        r0[x] = r
        d0[x] = KEEP * d0[x] + (inv0[odd] * (STEP * x_mask(0, x, gx0))) * r

    filter_planes(d0, w0, a0, 2, (bx + 12) // 2, rows0, lanes0)
    applied(a0, 4, (bx + 8) // 2, 0, use_step)
    out_ref[...] += d0[own0]

    def use_down(x, odd, av):
        r0[x] = (r0[x] - av) * (mask0 * x_mask(0, x, gx0))

    filter_planes(d0, w0, a0, 2, (bx + 10) // 2, rows0, lanes0)
    applied(a0, 4, (bx + 6) // 2, 0, use_down)

    def narrowed(ref, x):
        even = (
            ref[x] + 0.375 * (ref[x - 1] + ref[x + 1]) - 0.125 * (ref[x - 3] + ref[x + 3])
        )
        odd = ref[x + 2] + 0.75 * (ref[x + 1] + ref[x + 3])
        return even, odd

    coarse = []
    for q in range(cx // 2):
        for plane in narrowed(r0, H + 4 * q):
            coarse.append(exact(ry0[...], plane))
    rhs = zdot(jnp.concatenate(coarse, axis=0), rz0[...])
    wl = cz + 2 * ZR
    blk[...] = rhs.reshape(cx, cy, wl)

    if nz > 1:

        def gz_copies(off):
            k = int(off > 0)
            return [remote(blk, zin.at[k], gzsend.at[k], gzrecv.at[k], 2, off)]

        for off in both:
            start_if(2, off, gz_copies(off))
        for off in both:
            recv_if(2, off, gz_copies(off))
        wlane = lax.broadcasted_iota(jnp.int32, (cy, wl), 1)
        for p in range(cx):
            lower = pltpu.roll(zin[1, p], wl - cz, 1)
            upper = pltpu.roll(zin[0, p], cz, 1)
            zin[2, p] = jnp.where(
                wlane < ZR, lower, jnp.where(wlane >= ZR + cz, upper, blk[p])
            )
    else:
        zin[2] = blk[...]

    def slot(axis, off):
        if (full_x, full_y)[axis]:
            return (ix, iy)[axis]
        return REACH - off

    def spot(axis, off, size):
        return pl.ds(pl.multiple_of(slot(axis, off) * size, size), size)

    def gx_copies(off):
        k = off + REACH * 2
        dst = g1.at[spot(0, off, cx), spot(1, 0, cy)]
        return [remote(zin.at[2], dst, gsend.at[0, k], grecv.at[0, k], 0, off)]

    def gy_copies(off):
        k = off + REACH * 2
        src = g1.at[:, spot(1, 0, cy)]
        dst = g1.at[:, spot(1, off, cy)]
        return [remote(src, dst, gsend.at[1, k], grecv.at[1, k], 1, off)]

    for off in offsets[0]:
        start_if(0, off, gx_copies(off))
    g1[spot(0, 0, cx), spot(1, 0, cy)] = zin[2]
    rows1, planes1 = cy * wy + 8, cx * wx
    d1[...] = jnp.zeros_like(d1)
    a1[...] = jnp.zeros_like(a1)
    d2[...] = jnp.zeros_like(d2)
    a2[...] = jnp.zeros_like(a2)
    c1[...] = jnp.zeros_like(c1)
    r1[...] = jnp.zeros_like(r1)
    t2[...] = jnp.zeros_like(t2)
    for off in offsets[0]:
        recv_if(0, off, gx_copies(off))
    for off in offsets[1]:
        start_if(1, off, gy_copies(off))
    for off in offsets[1]:
        recv_if(1, off, gy_copies(off))

    Q = 8
    mask1, inv1 = masks_and_diagonals(
        1, rows1, wl, start_y * cy, cy * wy, lambda z: z, lambda z: z >= 0, iz * cz - ZR
    )
    gx1 = start_x * cx - Q

    def first_mid(p, carry):
        for odd in range(2):
            x = 2 * p + odd
            r = g1[x]
            r1[x + Q] = r
            d = (inv1[odd] * (FIRST * x_mask(1, x + Q, gx1))) * r
            d1[x + Q] = d
            s1[x] = d
        return carry

    lax.fori_loop(0, planes1 // 2, first_mid, 0)

    def use_step1(x, odd, av):
        r = r1[x] - av
        r1[x] = r
        d = KEEP * d1[x] + (inv1[odd] * (STEP * x_mask(1, x, gx1))) * r
        d1[x] = d
        s1[x - Q] += d

    def use_down1(x, odd, av):
        r1[x] = (r1[x] - av) * (mask1 * x_mask(1, x, gx1))

    half1 = planes1 // 2
    filter_planes(d1, w1, a1, Q, half1, rows1, wl)
    applied(a1, Q, half1, 1, use_step1)
    filter_planes(d1, w1, a1, Q, half1, rows1, wl)
    applied(a1, Q, half1, 1, use_down1)

    planes2 = planes1 // 2
    rows2 = cy * wy // 2 + 8
    mask2, inv2 = masks_and_diagonals(
        2, rows2, wl, start_y * (cy // 2), cy * wy // 2, lambda z: z,
        lambda z: z < wl // 2, iz * (cz // 2) - ZR // 2,
    )
    gx2 = start_x * (cx // 2) - Q

    def down_mid(q, carry):
        parts = [exact(ry1[...], plane) for plane in narrowed(r1, Q + 4 * q)]
        prod = zdot(jnp.concatenate(parts, axis=0), rz1[...])
        for odd in range(2):
            x = 2 * q + odd + Q
            r = prod[odd * rows2 : (odd + 1) * rows2]
            r2[x] = r
            d2[x] = (inv2[odd] * (FIRST * x_mask(2, x, gx2))) * r
        return carry

    lax.fori_loop(0, planes2 // 2, down_mid, 0)
    filter_planes(d2, w2, a2, Q, planes2 // 2, rows2, wl)

    def use_last(x, odd, av):
        r = r2[x] - av
        d2[x] = (1.0 + KEEP) * d2[x] + (inv2[odd] * (STEP * x_mask(2, x, gx2))) * r

    applied(a2, Q, planes2 // 2, 2, use_last)

    def up_last(p, carry):
        v = zdot(d2[pl.ds(Q + 2 * p, 2)].reshape(2 * rows2, wl), pz1[...])
        for k in range(2):
            t2[2 * p + k] = exact(py1[...], v[k * rows2 : (k + 1) * rows2])
        return carry

    lax.fori_loop(0, planes2 // 2, up_last, 0)

    def widened(ref, x):
        one, two, three = ref[x], ref[x + 1], ref[x + 2]
        return (
            one,
            0.375 * one + 0.75 * two - 0.125 * three,
            two,
            -0.125 * one + 0.75 * two + 0.375 * three,
        )

    def up_mid(q, carry):
        for k, plane in enumerate(widened(t2, 2 * q)):
            x = 4 * q + k
            e = plane * (mask1 * x_mask(1, x + Q, gx1))
            d1[x + Q] = e
            s1[x] += e
        return carry

    lax.fori_loop(0, planes1 // 4, up_mid, 0)
    filter_planes(d1, w1, a1, Q, half1, rows1, wl)

    def use_up1(x, odd, av):
        r = r1[x] - av
        r1[x] = r
        d = (inv1[odd] * (FIRST * x_mask(1, x, gx1))) * r
        d1[x] = d
        s1[x - Q] += d

    applied(a1, Q, half1, 1, use_up1)
    filter_planes(d1, w1, a1, Q, half1, rows1, wl)

    def use_final1(x, odd, av):
        r = r1[x] - av
        d = KEEP * d1[x] + (inv1[odd] * (STEP * x_mask(1, x, gx1))) * r
        c1[x, 8 : 8 + rows1] = s1[x - Q] + d

    applied(a1, Q, half1, 1, use_final1)

    crow = cy + 16
    own_x = (ix if full_x else REACH) * cx + Q
    own_y = pl.multiple_of((iy if full_y else REACH) * cy, 8)

    def up_first(p, carry):
        x = own_x - 2 + 2 * p
        v = c1[pl.ds(x, 2), pl.ds(own_y, crow)].reshape(2 * crow, wl)
        v = zdot(v, pz0[...])
        for k in range(2):
            c0[2 * p + k] = exact(py0[...], v[k * crow : (k + 1) * crow])
        return carry

    lax.fori_loop(0, (cx + 6) // 2, up_first, 0)

    def up_fine(q, carry):
        for k, plane in enumerate(widened(c0, 2 * q)):
            x = H - 4 + 4 * q + k
            d0[x] = plane * (mask0 * x_mask(0, x, gx0))
        return carry

    lax.fori_loop(0, (bx + 8) // 4, up_fine, 0)
    out_ref[...] += d0[own0]
    filter_planes(d0, w0, a0, 4, (bx + 8) // 2, rows0, lanes0)

    def use_up(x, odd, av):
        r = r0[x] - av
        r0[x] = r
        d0[x] = (inv0[odd] * (FIRST * x_mask(0, x, gx0))) * r

    applied(a0, 6, (bx + 4) // 2, 0, use_up)
    filter_planes(d0, w0, a0, 6, (bx + 4) // 2, rows0, lanes0)

    def use_final(x, odd, av):
        r = r0[x] - av
        d = d0[x]
        new = d + (KEEP * d + (inv0[odd] * STEP) * r)
        out_ref[x - H] += new[H : H + by, :bz]

    applied(a0, H, bx // 2, 0, use_final)

    for off in both:
        sent_if(0, off, x_copies(off))
        sent_if(1, off, y_copies(off) + corner_copies(off))
        if nz > 1:
            sent_if(2, off, z_copies(off) + gz_copies(off))
    for off in offsets[0]:
        sent_if(0, off, gx_copies(off))
    for off in offsets[1]:
        sent_if(1, off, gy_copies(off))


def local(mesh_shape, u, b):
    nx, ny, nz = (mesh_shape[a] for a in ("gx", "gy", "gz"))
    bx, by, bz = u.shape
    cx, cy, cz = bx // 2, by // 2, bz // 2
    wx = nx if nx <= 2 * REACH + 1 else 2 * REACH + 1
    wy = ny if ny <= 2 * REACH + 1 else 2 * REACH + 1
    wl = cz + 2 * ZR
    rows0, lanes0 = by + 2 * H, 2 * bz
    rows1, planes1 = cy * wy + 8, cx * wx
    rows2, planes2 = cy * wy // 2 + 8, planes1 // 2
    crow = cy + 16

    def z_pos(z):
        return z if z >= 0 else z + lanes0

    w0 = band_matrices(lanes0, True)
    w1 = band_matrices(wl, False)
    w2 = band_matrices(wl, False)
    rz0 = transfer(restrict_taps, range(cz), lambda o: o + ZR, z_pos, wl, lanes0, 2).T
    ry0 = transfer(restrict_taps, range(cy), lambda o: o, lambda f: f + H, cy, rows0, 2)
    rz1 = transfer(restrict_taps, range(wl // 2), lambda o: o, lambda f: f, wl, wl, 2).T
    live1 = lambda f: f if 0 <= f < cy * wy else None
    ry1 = transfer(restrict_taps, range(cy * wy // 2), lambda o: o, live1, rows2, rows1, 2)
    pz1 = transfer(prolong_taps, range(wl), lambda o: o, lambda c: c, wl, wl, 0).T
    live2 = lambda c: c if 0 <= c < cy * wy // 2 else None
    py1 = transfer(prolong_taps, range(cy * wy), lambda o: o, live2, rows1, rows2, 0)
    pz0 = transfer(
        prolong_taps, range(-H, bz + H), z_pos, lambda c: c + ZR, lanes0, wl, 0
    ).T
    py0 = transfer(
        prolong_taps, range(-H, by + H), lambda o: o + H, lambda c: c + 8, rows0, crow, 0
    )
    bf = lambda m: jnp.asarray(m, BF16)
    fl = lambda m: jnp.asarray(m, F32)
    consts = (
        bf(w0), bf(w1), bf(w2), bf(rz0), fl(ry0), bf(rz1), fl(ry1), bf(pz1), fl(py1),
        bf(pz0), fl(py0),
    )
    vm = lambda *s: pltpu.VMEM(s, F32)
    groups = (bx + 2 * H) // (bz // H)
    dma = lambda *s: pltpu.SemaphoreType.DMA(s)
    geo = (nx, ny, nz, bx, by, bz, wx, wy)
    return pl.pallas_call(
        functools.partial(kernel, geo),
        out_shape=jax.ShapeDtypeStruct(u.shape, F32),
        in_specs=[pl.BlockSpec(memory_space=pltpu.VMEM)] * (2 + len(consts)),
        out_specs=pl.BlockSpec(memory_space=pltpu.VMEM),
        scratch_shapes=[
            vm(bx + 16, rows0, lanes0), vm(bx + 16, rows0, lanes0),
            vm(bx + 16, rows0, lanes0), vm(bx + 16, rows0, lanes0),
            vm(2, bx + 16, rows0, lanes0), vm(cx + 8, rows0, lanes0),
            vm(2, 2, groups, rows0, bz), vm(2, 2, groups, rows0, bz),
            vm(cx, cy, wl), vm(3, cx, cy, wl),
            vm(planes1, rows1, wl), vm(planes1 + 16, rows1, wl),
            vm(planes1 + 16, rows1, wl), vm(planes1, rows1, wl),
            vm(2, planes1 + 16, rows1, wl), vm(planes1 + 16, rows1 + 8, wl),
            vm(planes2 + 16, rows2, wl), vm(planes2 + 16, rows2, wl),
            vm(2, planes2 + 16, rows2, wl), vm(planes2 + 8, rows1, wl),
            dma(16), dma(16), dma(2), dma(2),
            dma(2, 4 * REACH + 1), dma(2, 4 * REACH + 1), dma(2), dma(2),
        ],
        compiler_params=pltpu.CompilerParams(
            collective_id=0, has_side_effects=True, vmem_limit_bytes=60 * 1024 * 1024
        ),
    )(u, b, *consts)


def solution(mesh):
    placed = P("gx", "gy", "gz")
    return jax.shard_map(
        functools.partial(local, dict(mesh.shape)), mesh=mesh,
        in_specs=(placed, placed), out_specs=placed, check_vma=False,
    )
```

```python
import functools

import jax
import jax.numpy as jnp
import numpy as np
from jax import lax
from jax.experimental import pallas as pl
from jax.experimental.pallas import tpu as pltpu
from jax.sharding import PartitionSpec as P

F32 = jnp.float32
BF16 = jnp.bfloat16
MESH = pl.DeviceIdType.MESH
H = 8
ZR = 32
REACH = 3

RHO0 = 1.0 / 1.2
RHO1 = 1.0 / (2.4 - RHO0)
FIRST = 1.0 / 1.32
KEEP = RHO1 * RHO0
STEP = 2.0 * RHO1 / 1.1


def restrict_taps(g):
    if g % 2 == 0:
        return ((-3, -0.125), (-1, 0.375), (0, 1.0), (1, 0.375), (3, -0.125))
    return ((-1, 0.75), (0, 1.0), (1, 0.75))


def prolong_taps(f):
    if f % 2 == 0:
        return ((f // 2, 1.0),)
    q = f // 4
    if f % 4 == 1:
        return ((2 * q, 0.375), (2 * q + 1, 0.75), (2 * q + 2, -0.125))
    return ((2 * q, -0.125), (2 * q + 1, 0.75), (2 * q + 2, 0.375))


def transfer(taps, outs, out_pos, in_pos, n_out, n_in, scale):
    m = np.zeros((n_out, n_in), np.float32)
    for o in outs:
        for s, w in taps(o):
            row, col = out_pos(o), in_pos(scale * o + s if scale else s)
            if col is not None and 0 <= col < n_in:
                m[row, col] += w
    return m


def zdot(v, w):
    hi = v.astype(BF16)
    lo = (v - hi.astype(F32)).astype(BF16)
    return jnp.dot(hi, w, preferred_element_type=F32) + jnp.dot(
        lo, w, preferred_element_type=F32
    )


def exact(a, b):
    return jnp.dot(a, b, preferred_element_type=F32, precision=lax.Precision.HIGHEST)


def z_filters(v):
    lanes = v.shape[1]
    even = lax.broadcasted_iota(jnp.int32, v.shape, 1) % 2 == 0
    s1 = pltpu.roll(v, 1, 1) + pltpu.roll(v, lanes - 1, 1)
    s2 = jnp.where(even, pltpu.roll(v, 2, 1) + pltpu.roll(v, lanes - 2, 1), 0.0)
    md = jnp.where(even, 8.0, 16.0)
    kd = jnp.where(even, 14.0, 16.0)
    return md * v + 2.0 * s1 - s2, kd * v - 8.0 * s1 + s2


def y_filters(mz, kz):
    rows = mz.shape[0]
    even = lax.broadcasted_iota(jnp.int32, mz.shape, 0) % 2 == 0

    def sums(v):
        s1 = pltpu.roll(v, 1, 0) + pltpu.roll(v, rows - 1, 0)
        s2 = pltpu.roll(v, 2, 0) + pltpu.roll(v, rows - 2, 0)
        return s1, jnp.where(even, s2, 0.0)

    m1, m2 = sums(mz)
    k1, k2 = sums(kz)
    md = jnp.where(even, 8.0, 16.0)
    kd = jnp.where(even, 14.0, 16.0)
    first = md * mz + 2.0 * m1 - m2
    second = (kd * mz - 8.0 * m1 + m2) + (md * kz + 2.0 * k1 - k2)
    return first, second


def kernel(
    geo, u_ref, b_ref, rz0, ry0, rz1, ry1, pz1, py1, pz0, py0, out_ref,
    ue, be, d0, r0, a0, c0, packs, unpacks, blk, zin, g1, d1, r1, s1, a1, c1,
    r2, d2, a2, t2, send, recv, zsend, zrecv, gsend, grecv, gzsend, gzrecv,
):
    nx, ny, nz, bx, by, bz, wx, wy = geo
    ix, iy, iz = lax.axis_index("gx"), lax.axis_index("gy"), lax.axis_index("gz")
    full_x, full_y = wx == nx, wy == ny
    cx, cy, cz = bx // 2, by // 2, bz // 2
    start_x = 0 if full_x else ix - REACH
    start_y = 0 if full_y else iy - REACH

    def at(axis, off):
        return (
            ix + off if axis == 0 else ix,
            iy + off if axis == 1 else iy,
            iz + off if axis == 2 else iz,
        )

    place = (ix, iy, iz)
    counts = (nx, ny, nz)

    def there(axis, off):
        pos = place[axis] + off
        return (pos >= 0) & (pos < counts[axis])

    spans = (wx - 1 if full_x else REACH, wy - 1 if full_y else REACH, 1 if nz > 1 else 0)
    offsets = [[o for o in range(-s, s + 1) if o] for s in spans]

    ue[...] = jnp.zeros_like(ue)
    be[...] = jnp.zeros_like(be)
    unpacks[...] = jnp.zeros_like(unpacks)
    zin[...] = jnp.zeros_like(zin)
    g1[...] = jnp.zeros_like(g1)
    ue[H : H + bx, H : H + by, :bz] = u_ref[...]
    be[H : H + bx, H : H + by, :bz] = b_ref[...]

    barrier = pltpu.get_barrier_semaphore()
    total = 0
    for axis in range(3):
        for off in offsets[axis]:
            ok = there(axis, off)
            total = total + ok.astype(jnp.int32)

            @pl.when(ok)
            def _():
                pl.semaphore_signal(
                    barrier, inc=1, device_id=at(axis, off), device_id_type=MESH
                )

    pl.semaphore_wait(barrier, total)

    def remote(src, dst, ss, rs, axis, off):
        return pltpu.make_async_remote_copy(
            src_ref=src, dst_ref=dst, send_sem=ss, recv_sem=rs,
            device_id=at(axis, off), device_id_type=MESH,
        )

    def start_if(axis, off, copies):
        @pl.when(there(axis, off))
        def _():
            for c in copies:
                c.start()

    def recv_if(axis, off, copies):
        @pl.when(there(axis, -off))
        def _():
            for c in copies:
                c.wait_recv()

    def sent_if(axis, off, copies):
        @pl.when(there(axis, off))
        def _():
            for c in copies:
                c.wait_send()

    L = bz

    def x_copies(off):
        res = []
        for n, (ref, ext, w) in enumerate(((u_ref, ue, H), (b_ref, be, H - 2))):
            k = n * 2 + (off > 0)
            lo = bx - w if off > 0 else 0
            dst = H - w if off > 0 else H + bx
            res.append(
                remote(
                    ref.at[lo : lo + w],
                    ext.at[dst : dst + w, H : H + by, :L],
                    send.at[k], recv.at[k], 0, off,
                )
            )
        return res

    def y_copies(off):
        res = []
        for n, (ref, ext) in enumerate(((u_ref, ue), (b_ref, be))):
            k = 4 + n * 2 + (off > 0)
            lo = by - H if off > 0 else 0
            dst = 0 if off > 0 else H + by
            res.append(
                remote(
                    ref.at[:, lo : lo + H],
                    ext.at[H : H + bx, dst : dst + H, :L],
                    send.at[k], recv.at[k], 1, off,
                )
            )
        return res

    def corner_copies(off):
        res = []
        for n, (ext, w) in enumerate(((ue, H), (be, H - 2))):
            for side in range(2):
                k = 8 + n * 4 + side * 2 + (off > 0)
                xs = H - w if side == 0 else H + bx
                lo = by if off > 0 else H
                dst = 0 if off > 0 else H + by
                res.append(
                    remote(
                        ext.at[xs : xs + w, lo : lo + H, :L],
                        ext.at[xs : xs + w, dst : dst + H, :L],
                        send.at[k], recv.at[k], 1, off,
                    )
                )
        return res

    both = (-1, 1)
    for off in both:
        start_if(0, off, x_copies(off))
    for off in both:
        start_if(1, off, y_copies(off))
    for off in both:
        recv_if(0, off, x_copies(off))
    for off in both:
        start_if(1, off, corner_copies(off))
    for off in both:
        recv_if(1, off, y_copies(off) + corner_copies(off))

    per = L // H
    lane = lax.broadcasted_iota(jnp.int32, (by + 2 * H, L), 1)
    groups = (bx + 2 * H) // per
    if nz > 1:
        for n, ext in enumerate((ue, be)):
            for g in range(groups):
                low = jnp.zeros((by + 2 * H, L), F32)
                high = jnp.zeros((by + 2 * H, L), F32)
                for k in range(per):
                    plane = ext[g * per + k, :, :L]
                    here = (lane // H) == k
                    low = jnp.where(here, pltpu.roll(plane, (k * H) % L, 1), low)
                    high = jnp.where(here, pltpu.roll(plane, ((k + 1) * H) % L, 1), high)
                packs[0, n, g] = low
                packs[1, n, g] = high

        def z_copies(off):
            k = int(off > 0)
            return [remote(packs.at[k], unpacks.at[k], zsend.at[k], zrecv.at[k], 2, off)]

        for off in both:
            start_if(2, off, z_copies(off))
        for off in both:
            recv_if(2, off, z_copies(off))
        for n, ext in enumerate((ue, be)):
            for g in range(groups):
                upper, lower = unpacks[0, n, g], unpacks[1, n, g]
                for k in range(per):
                    up = pltpu.roll(upper, (L - k * H) % L, 1)
                    lo = pltpu.roll(lower, (L - (k + 1) * H) % L, 1)
                    ext[g * per + k, :, L:] = jnp.where(
                        lane < H, up, jnp.where(lane >= L - H, lo, 0.0)
                    )

    def masks_and_diagonals(level, rows, lanes, y_first, y_end, z_of_lane, z_ok, z_first):
        yy = lax.broadcasted_iota(jnp.int32, (rows, lanes), 0)
        zz = lax.broadcasted_iota(jnp.int32, (rows, lanes), 1)
        y_even, z_even = yy % 2 == 0, zz % 2 == 0
        gy = y_first + yy
        gz = z_first + z_of_lane(zz)
        n_y, n_z = (ny * by) >> level, (nz * bz) >> level
        ok = (gy >= 0) & (gy < n_y) & (yy < y_end) & (gz >= 0) & (gz < n_z) & z_ok(zz)
        mask = jnp.where(ok, 1.0, 0.0)
        my = jnp.where(y_even, 8.0, 16.0) / 30.0
        mz = jnp.where(z_even, 8.0, 16.0) / 30.0
        ky = jnp.where(y_even, 14.0, 16.0) / 3.0
        kz = jnp.where(z_even, 14.0, 16.0) / 3.0
        inv = []
        for kx, mx in ((14.0 / 3.0, 8.0 / 30.0), (16.0 / 3.0, 16.0 / 30.0)):
            diag = 2.0**level * (kx * my * mz + mx * ky * mz + mx * my * kz)
            inv.append(mask / diag)
        return mask, inv

    def filter_planes(src, acc, first, pairs):
        def body(p, carry):
            x = first + 2 * p
            for k in range(2):
                a, c = y_filters(*z_filters(src[x + k]))
                acc[0, x + k] = a
                acc[1, x + k] = c
            return carry

        lax.fori_loop(0, pairs, body, 0)

    def applied(acc, first, pairs, level, use):
        scale = 2.0**level / 2700.0

        def body(p, carry):
            x = first + 2 * p
            for t in range(acc.shape[2] // 8):
                y = slice(8 * t, 8 * t + 8)
                a = [acc[0, x + k, y] for k in range(-2, 4)]
                c = [acc[1, x + k, y] for k in range(-2, 4)]
                even = (14.0 * a[2] - 8.0 * (a[1] + a[3]) + (a[0] + a[4])) + (
                    8.0 * c[2] + 2.0 * (c[1] + c[3]) - (c[0] + c[4])
                )
                odd = (16.0 * a[3] - 8.0 * (a[2] + a[4])) + (
                    16.0 * c[3] + 2.0 * (c[2] + c[4])
                )
                use(x, 0, scale * even, t)
                use(x + 1, 1, scale * odd, t)
            return carry

        lax.fori_loop(0, pairs, body, 0)

    rows0, lanes0 = by + 2 * H, 2 * bz
    mask0, inv0 = masks_and_diagonals(
        0, rows0, lanes0, iy * by - H, rows0,
        lambda z: jnp.where(z < bz + bz // 2, z, z - 2 * bz), lambda z: z >= 0, iz * bz,
    )

    def x_mask(level, x, x_first):
        g = x_first + x
        return jnp.where((g >= 0) & (g < ((nx * bx) >> level)), 1.0, 0.0).astype(F32)

    gx0 = ix * bx - H

    def tile(t):
        return slice(8 * t, 8 * t + 8)

    def use_residual(x, odd, av, t):
        y = tile(t)
        r = be[x, y] - av
        r0[x, y] = r
        d0[x, y] = (inv0[odd][y] * (FIRST * x_mask(0, x, gx0))) * r

    filter_planes(ue, a0, 0, (bx + 16) // 2)
    applied(a0, 2, (bx + 12) // 2, 0, use_residual)
    own0 = (slice(H, H + bx), slice(H, H + by), slice(0, bz))
    out_ref[...] = u_ref[...] + d0[own0]

    def use_step(x, odd, av, t):
        y = tile(t)
        r = r0[x, y] - av
        r0[x, y] = r
        d0[x, y] = KEEP * d0[x, y] + (inv0[odd][y] * (STEP * x_mask(0, x, gx0))) * r

    filter_planes(d0, a0, 2, (bx + 12) // 2)
    applied(a0, 4, (bx + 8) // 2, 0, use_step)
    out_ref[...] += d0[own0]

    def use_down(x, odd, av, t):
        y = tile(t)
        r0[x, y] = (r0[x, y] - av) * (mask0[y] * x_mask(0, x, gx0))

    filter_planes(d0, a0, 2, (bx + 10) // 2)
    applied(a0, 4, (bx + 6) // 2, 0, use_down)

    def narrowed(ref, x):
        even = (
            ref[x] + 0.375 * (ref[x - 1] + ref[x + 1]) - 0.125 * (ref[x - 3] + ref[x + 3])
        )
        odd = ref[x + 2] + 0.75 * (ref[x + 1] + ref[x + 3])
        return even, odd

    coarse = []
    for q in range(cx // 2):
        for plane in narrowed(r0, H + 4 * q):
            coarse.append(exact(ry0[...], plane))
    rhs = zdot(jnp.concatenate(coarse, axis=0), rz0[...])
    wl = cz + 2 * ZR
    blk[...] = rhs.reshape(cx, cy, wl)

    if nz > 1:

        def gz_copies(off):
            k = int(off > 0)
            return [remote(blk, zin.at[k], gzsend.at[k], gzrecv.at[k], 2, off)]

        for off in both:
            start_if(2, off, gz_copies(off))
        for off in both:
            recv_if(2, off, gz_copies(off))
        wlane = lax.broadcasted_iota(jnp.int32, (cy, wl), 1)
        for p in range(cx):
            lower = pltpu.roll(zin[1, p], wl - cz, 1)
            upper = pltpu.roll(zin[0, p], cz, 1)
            zin[2, p] = jnp.where(
                wlane < ZR, lower, jnp.where(wlane >= ZR + cz, upper, blk[p])
            )
    else:
        zin[2] = blk[...]

    def slot(axis, off):
        if (full_x, full_y)[axis]:
            return (ix, iy)[axis]
        return REACH - off

    def spot(axis, off, size):
        return pl.ds(pl.multiple_of(slot(axis, off) * size, size), size)

    def gx_copies(off):
        k = off + REACH * 2
        dst = g1.at[spot(0, off, cx), spot(1, 0, cy)]
        return [remote(zin.at[2], dst, gsend.at[0, k], grecv.at[0, k], 0, off)]

    def gy_copies(off):
        k = off + REACH * 2
        src = g1.at[:, spot(1, 0, cy)]
        dst = g1.at[:, spot(1, off, cy)]
        return [remote(src, dst, gsend.at[1, k], grecv.at[1, k], 1, off)]

    for off in offsets[0]:
        start_if(0, off, gx_copies(off))
    g1[spot(0, 0, cx), spot(1, 0, cy)] = zin[2]
    rows1, planes1 = cy * wy + 8, cx * wx
    d1[...] = jnp.zeros_like(d1)
    a1[...] = jnp.zeros_like(a1)
    d2[...] = jnp.zeros_like(d2)
    a2[...] = jnp.zeros_like(a2)
    c1[...] = jnp.zeros_like(c1)
    r1[...] = jnp.zeros_like(r1)
    t2[...] = jnp.zeros_like(t2)
    for off in offsets[0]:
        recv_if(0, off, gx_copies(off))
    for off in offsets[1]:
        start_if(1, off, gy_copies(off))
    for off in offsets[1]:
        recv_if(1, off, gy_copies(off))

    Q = 8
    mask1, inv1 = masks_and_diagonals(
        1, rows1, wl, start_y * cy, cy * wy, lambda z: z, lambda z: z >= 0, iz * cz - ZR
    )
    gx1 = start_x * cx - Q

    def first_mid(p, carry):
        for odd in range(2):
            x = 2 * p + odd
            r = g1[x]
            r1[x + Q] = r
            d = (inv1[odd] * (FIRST * x_mask(1, x + Q, gx1))) * r
            d1[x + Q] = d
            s1[x] = d
        return carry

    lax.fori_loop(0, planes1 // 2, first_mid, 0)

    def use_step1(x, odd, av, t):
        y = tile(t)
        r = r1[x, y] - av
        r1[x, y] = r
        d = KEEP * d1[x, y] + (inv1[odd][y] * (STEP * x_mask(1, x, gx1))) * r
        d1[x, y] = d
        s1[x - Q, y] += d

    def use_down1(x, odd, av, t):
        y = tile(t)
        r1[x, y] = (r1[x, y] - av) * (mask1[y] * x_mask(1, x, gx1))

    half1 = planes1 // 2
    filter_planes(d1, a1, Q, half1)
    applied(a1, Q, half1, 1, use_step1)
    filter_planes(d1, a1, Q, half1)
    applied(a1, Q, half1, 1, use_down1)

    planes2 = planes1 // 2
    rows2 = cy * wy // 2 + 8
    mask2, inv2 = masks_and_diagonals(
        2, rows2, wl, start_y * (cy // 2), cy * wy // 2, lambda z: z,
        lambda z: z < wl // 2, iz * (cz // 2) - ZR // 2,
    )
    gx2 = start_x * (cx // 2) - Q

    def down_mid(q, carry):
        parts = [exact(ry1[...], plane) for plane in narrowed(r1, Q + 4 * q)]
        prod = zdot(jnp.concatenate(parts, axis=0), rz1[...])
        for odd in range(2):
            x = 2 * q + odd + Q
            r = prod[odd * rows2 : (odd + 1) * rows2]
            r2[x] = r
            d2[x] = (inv2[odd] * (FIRST * x_mask(2, x, gx2))) * r
        return carry

    lax.fori_loop(0, planes2 // 2, down_mid, 0)
    filter_planes(d2, a2, Q, planes2 // 2)

    def use_last(x, odd, av, t):
        y = tile(t)
        r = r2[x, y] - av
        step = (inv2[odd][y] * (STEP * x_mask(2, x, gx2))) * r
        d2[x, y] = (1.0 + KEEP) * d2[x, y] + step

    applied(a2, Q, planes2 // 2, 2, use_last)

    def up_last(p, carry):
        v = zdot(d2[pl.ds(Q + 2 * p, 2)].reshape(2 * rows2, wl), pz1[...])
        for k in range(2):
            t2[2 * p + k] = exact(py1[...], v[k * rows2 : (k + 1) * rows2])
        return carry

    lax.fori_loop(0, planes2 // 2, up_last, 0)

    def widened(ref, x):
        one, two, three = ref[x], ref[x + 1], ref[x + 2]
        return (
            one,
            0.375 * one + 0.75 * two - 0.125 * three,
            two,
            -0.125 * one + 0.75 * two + 0.375 * three,
        )

    def up_mid(q, carry):
        for k, plane in enumerate(widened(t2, 2 * q)):
            x = 4 * q + k
            e = plane * (mask1 * x_mask(1, x + Q, gx1))
            d1[x + Q] = e
            s1[x] += e
        return carry

    lax.fori_loop(0, planes1 // 4, up_mid, 0)
    filter_planes(d1, a1, Q, half1)

    def use_up1(x, odd, av, t):
        y = tile(t)
        r = r1[x, y] - av
        r1[x, y] = r
        d = (inv1[odd][y] * (FIRST * x_mask(1, x, gx1))) * r
        d1[x, y] = d
        s1[x - Q, y] += d

    applied(a1, Q, half1, 1, use_up1)
    filter_planes(d1, a1, Q, half1)

    def use_final1(x, odd, av, t):
        y = tile(t)
        r = r1[x, y] - av
        d = KEEP * d1[x, y] + (inv1[odd][y] * (STEP * x_mask(1, x, gx1))) * r
        c1[x, tile(t + 1)] = s1[x - Q, y] + d

    applied(a1, Q, half1, 1, use_final1)

    crow = cy + 16
    own_x = (ix if full_x else REACH) * cx + Q
    own_y = pl.multiple_of((iy if full_y else REACH) * cy, 8)

    def up_first(p, carry):
        x = own_x - 2 + 2 * p
        v = c1[pl.ds(x, 2), pl.ds(own_y, crow)].reshape(2 * crow, wl)
        v = zdot(v, pz0[...])
        for k in range(2):
            c0[2 * p + k] = exact(py0[...], v[k * crow : (k + 1) * crow])
        return carry

    lax.fori_loop(0, (cx + 6) // 2, up_first, 0)

    def up_fine(q, carry):
        for k, plane in enumerate(widened(c0, 2 * q)):
            x = H - 4 + 4 * q + k
            d0[x] = plane * (mask0 * x_mask(0, x, gx0))
        return carry

    lax.fori_loop(0, (bx + 8) // 4, up_fine, 0)
    out_ref[...] += d0[own0]
    filter_planes(d0, a0, 4, (bx + 8) // 2)

    def use_up(x, odd, av, t):
        y = tile(t)
        r = r0[x, y] - av
        r0[x, y] = r
        d0[x, y] = (inv0[odd][y] * (FIRST * x_mask(0, x, gx0))) * r

    applied(a0, 6, (bx + 4) // 2, 0, use_up)
    filter_planes(d0, a0, 6, (bx + 4) // 2)

    def use_final(x, odd, av, t):
        if t == 0 or t == by // 8 + 1:
            return
        y = tile(t)
        r = r0[x, y] - av
        d = d0[x, y]
        new = d + (KEEP * d + (inv0[odd][y] * STEP) * r)
        out_ref[x - H, tile(t - 1)] += new[:, :bz]

    applied(a0, H, bx // 2, 0, use_final)

    for off in both:
        sent_if(0, off, x_copies(off))
        sent_if(1, off, y_copies(off) + corner_copies(off))
        if nz > 1:
            sent_if(2, off, z_copies(off) + gz_copies(off))
    for off in offsets[0]:
        sent_if(0, off, gx_copies(off))
    for off in offsets[1]:
        sent_if(1, off, gy_copies(off))


def local(mesh_shape, u, b):
    nx, ny, nz = (mesh_shape[a] for a in ("gx", "gy", "gz"))
    bx, by, bz = u.shape
    cx, cy, cz = bx // 2, by // 2, bz // 2
    wx = nx if nx <= 2 * REACH + 1 else 2 * REACH + 1
    wy = ny if ny <= 2 * REACH + 1 else 2 * REACH + 1
    wl = cz + 2 * ZR
    rows0, lanes0 = by + 2 * H, 2 * bz
    rows1, planes1 = cy * wy + 8, cx * wx
    rows2, planes2 = cy * wy // 2 + 8, planes1 // 2
    crow = cy + 16

    def z_pos(z):
        return z if z >= 0 else z + lanes0

    rz0 = transfer(restrict_taps, range(cz), lambda o: o + ZR, z_pos, wl, lanes0, 2).T
    ry0 = transfer(restrict_taps, range(cy), lambda o: o, lambda f: f + H, cy, rows0, 2)
    rz1 = transfer(restrict_taps, range(wl // 2), lambda o: o, lambda f: f, wl, wl, 2).T
    live1 = lambda f: f if 0 <= f < cy * wy else None
    ry1 = transfer(restrict_taps, range(cy * wy // 2), lambda o: o, live1, rows2, rows1, 2)
    pz1 = transfer(prolong_taps, range(wl), lambda o: o, lambda c: c, wl, wl, 0).T
    live2 = lambda c: c if 0 <= c < cy * wy // 2 else None
    py1 = transfer(prolong_taps, range(cy * wy), lambda o: o, live2, rows1, rows2, 0)
    pz0 = transfer(
        prolong_taps, range(-H, bz + H), z_pos, lambda c: c + ZR, lanes0, wl, 0
    ).T
    py0 = transfer(
        prolong_taps, range(-H, by + H), lambda o: o + H, lambda c: c + 8, rows0, crow, 0
    )
    bf = lambda m: jnp.asarray(m, BF16)
    fl = lambda m: jnp.asarray(m, F32)
    consts = (
        bf(rz0), fl(ry0), bf(rz1), fl(ry1), bf(pz1), fl(py1),
        bf(pz0), fl(py0),
    )
    vm = lambda *s: pltpu.VMEM(s, F32)
    groups = (bx + 2 * H) // (bz // H)
    dma = lambda *s: pltpu.SemaphoreType.DMA(s)
    geo = (nx, ny, nz, bx, by, bz, wx, wy)
    return pl.pallas_call(
        functools.partial(kernel, geo),
        out_shape=jax.ShapeDtypeStruct(u.shape, F32),
        in_specs=[pl.BlockSpec(memory_space=pltpu.VMEM)] * (2 + len(consts)),
        out_specs=pl.BlockSpec(memory_space=pltpu.VMEM),
        scratch_shapes=[
            vm(bx + 16, rows0, lanes0), vm(bx + 16, rows0, lanes0),
            vm(bx + 16, rows0, lanes0), vm(bx + 16, rows0, lanes0),
            vm(2, bx + 16, rows0, lanes0), vm(cx + 8, rows0, lanes0),
            vm(2, 2, groups, rows0, bz), vm(2, 2, groups, rows0, bz),
            vm(cx, cy, wl), vm(3, cx, cy, wl),
            vm(planes1, rows1, wl), vm(planes1 + 16, rows1, wl),
            vm(planes1 + 16, rows1, wl), vm(planes1, rows1, wl),
            vm(2, planes1 + 16, rows1, wl), vm(planes1 + 16, rows1 + 8, wl),
            vm(planes2 + 16, rows2, wl), vm(planes2 + 16, rows2, wl),
            vm(2, planes2 + 16, rows2, wl), vm(planes2 + 8, rows1, wl),
            dma(16), dma(16), dma(2), dma(2),
            dma(2, 4 * REACH + 1), dma(2, 4 * REACH + 1), dma(2), dma(2),
        ],
        compiler_params=pltpu.CompilerParams(
            collective_id=0, has_side_effects=True, vmem_limit_bytes=60 * 1024 * 1024
        ),
    )(u, b, *consts)


def solution(mesh):
    placed = P("gx", "gy", "gz")
    return jax.shard_map(
        functools.partial(local, dict(mesh.shape)), mesh=mesh,
        in_specs=(placed, placed), out_specs=placed, check_vma=False,
    )
```

```python
import functools

import jax
import jax.numpy as jnp
import numpy as np
from jax import lax
from jax.experimental import pallas as pl
from jax.experimental.pallas import tpu as pltpu
from jax.sharding import PartitionSpec as P

F32 = jnp.float32
BF16 = jnp.bfloat16
MESH = pl.DeviceIdType.MESH
H = 8
ZR = 32
REACH = 3

RHO0 = 1.0 / 1.2
RHO1 = 1.0 / (2.4 - RHO0)
FIRST = 1.0 / 1.32
KEEP = RHO1 * RHO0
STEP = 2.0 * RHO1 / 1.1


def restrict_taps(g):
    if g % 2 == 0:
        return ((-3, -0.125), (-1, 0.375), (0, 1.0), (1, 0.375), (3, -0.125))
    return ((-1, 0.75), (0, 1.0), (1, 0.75))


def prolong_taps(f):
    if f % 2 == 0:
        return ((f // 2, 1.0),)
    q = f // 4
    if f % 4 == 1:
        return ((2 * q, 0.375), (2 * q + 1, 0.75), (2 * q + 2, -0.125))
    return ((2 * q, -0.125), (2 * q + 1, 0.75), (2 * q + 2, 0.375))


def transfer(taps, outs, out_pos, in_pos, n_out, n_in, scale):
    m = np.zeros((n_out, n_in), np.float32)
    for o in outs:
        for s, w in taps(o):
            row, col = out_pos(o), in_pos(scale * o + s if scale else s)
            if col is not None and 0 <= col < n_in:
                m[row, col] += w
    return m


def zdot(v, w):
    hi = v.astype(BF16)
    lo = (v - hi.astype(F32)).astype(BF16)
    return jnp.dot(hi, w, preferred_element_type=F32) + jnp.dot(
        lo, w, preferred_element_type=F32
    )


def exact(a, b):
    return jnp.dot(a, b, preferred_element_type=F32, precision=lax.Precision.HIGHEST)


def z_filters(v):
    lanes = v.shape[1]
    even = lax.broadcasted_iota(jnp.int32, v.shape, 1) % 2 == 0
    s1 = pltpu.roll(v, 1, 1) + pltpu.roll(v, lanes - 1, 1)
    s2 = jnp.where(even, pltpu.roll(v, 2, 1) + pltpu.roll(v, lanes - 2, 1), 0.0)
    m = jnp.where(even, 8.0, 16.0) * v + 2.0 * s1 - s2
    w = jnp.where(even, -2.0, -16.0) * v - 12.0 * s1 + 3.0 * s2
    return m, w


def kernel(
    geo, u_ref, b_ref, rz0, ry0, rz1, ry1, pz1, py1, pz0, py0, out_ref,
    ue, be, d0, r0, a0, c0, packs, unpacks, y0, y1, y2, blk, zin, g1, d1, r1, s1, a1, c1,
    r2, d2, a2, t2, send, recv, zsend, zrecv, gsend, grecv, gzsend, gzrecv,
):
    nx, ny, nz, bx, by, bz, wx, wy = geo
    ix, iy, iz = lax.axis_index("gx"), lax.axis_index("gy"), lax.axis_index("gz")
    full_x, full_y = wx == nx, wy == ny
    cx, cy, cz = bx // 2, by // 2, bz // 2
    start_x = 0 if full_x else ix - REACH
    start_y = 0 if full_y else iy - REACH

    def at(axis, off):
        return (
            ix + off if axis == 0 else ix,
            iy + off if axis == 1 else iy,
            iz + off if axis == 2 else iz,
        )

    place = (ix, iy, iz)
    counts = (nx, ny, nz)

    def there(axis, off):
        pos = place[axis] + off
        return (pos >= 0) & (pos < counts[axis])

    spans = (wx - 1 if full_x else REACH, wy - 1 if full_y else REACH, 1 if nz > 1 else 0)
    offsets = [[o for o in range(-s, s + 1) if o] for s in spans]

    ue[...] = jnp.zeros_like(ue)
    be[...] = jnp.zeros_like(be)
    unpacks[...] = jnp.zeros_like(unpacks)
    y0[...] = jnp.zeros_like(y0)
    zin[...] = jnp.zeros_like(zin)
    g1[...] = jnp.zeros_like(g1)
    ue[H : H + bx, H : H + by, :bz] = u_ref[...]
    be[H : H + bx, H : H + by, :bz] = b_ref[...]

    barrier = pltpu.get_barrier_semaphore()
    total = 0
    for axis in range(3):
        for off in offsets[axis]:
            ok = there(axis, off)
            total = total + ok.astype(jnp.int32)

            @pl.when(ok)
            def _():
                pl.semaphore_signal(
                    barrier, inc=1, device_id=at(axis, off), device_id_type=MESH
                )

    pl.semaphore_wait(barrier, total)

    def remote(src, dst, ss, rs, axis, off):
        return pltpu.make_async_remote_copy(
            src_ref=src, dst_ref=dst, send_sem=ss, recv_sem=rs,
            device_id=at(axis, off), device_id_type=MESH,
        )

    def start_if(axis, off, copies):
        @pl.when(there(axis, off))
        def _():
            for c in copies:
                c.start()

    def recv_if(axis, off, copies):
        @pl.when(there(axis, -off))
        def _():
            for c in copies:
                c.wait_recv()

    def sent_if(axis, off, copies):
        @pl.when(there(axis, off))
        def _():
            for c in copies:
                c.wait_send()

    L = bz

    def x_copies(off):
        res = []
        for n, (ref, ext, w) in enumerate(((u_ref, ue, H), (b_ref, be, H - 2))):
            k = n * 2 + (off > 0)
            lo = bx - w if off > 0 else 0
            dst = H - w if off > 0 else H + bx
            res.append(
                remote(
                    ref.at[lo : lo + w],
                    ext.at[dst : dst + w, H : H + by, :L],
                    send.at[k], recv.at[k], 0, off,
                )
            )
        return res

    def y_copies(off):
        res = []
        for n, (ref, ext) in enumerate(((u_ref, ue), (b_ref, be))):
            k = 4 + n * 2 + (off > 0)
            lo = by - H if off > 0 else 0
            dst = 0 if off > 0 else H + by
            res.append(
                remote(
                    ref.at[:, lo : lo + H],
                    ext.at[H : H + bx, dst : dst + H, :L],
                    send.at[k], recv.at[k], 1, off,
                )
            )
        return res

    def corner_copies(off):
        res = []
        for n, (ext, w) in enumerate(((ue, H), (be, H - 2))):
            for side in range(2):
                k = 8 + n * 4 + side * 2 + (off > 0)
                xs = H - w if side == 0 else H + bx
                lo = by if off > 0 else H
                dst = 0 if off > 0 else H + by
                res.append(
                    remote(
                        ext.at[xs : xs + w, lo : lo + H, :L],
                        ext.at[xs : xs + w, dst : dst + H, :L],
                        send.at[k], recv.at[k], 1, off,
                    )
                )
        return res

    both = (-1, 1)
    for off in both:
        start_if(0, off, x_copies(off))
    for off in both:
        start_if(1, off, y_copies(off))
    for off in both:
        recv_if(0, off, x_copies(off))
    for off in both:
        start_if(1, off, corner_copies(off))
    for off in both:
        recv_if(1, off, y_copies(off) + corner_copies(off))

    per = L // H
    lane = lax.broadcasted_iota(jnp.int32, (by + 2 * H, L), 1)
    groups = (bx + 2 * H) // per
    if nz > 1:
        for n, ext in enumerate((ue, be)):
            for g in range(groups):
                low = jnp.zeros((by + 2 * H, L), F32)
                high = jnp.zeros((by + 2 * H, L), F32)
                for k in range(per):
                    plane = ext[g * per + k, :, :L]
                    here = (lane // H) == k
                    low = jnp.where(here, pltpu.roll(plane, (k * H) % L, 1), low)
                    high = jnp.where(here, pltpu.roll(plane, ((k + 1) * H) % L, 1), high)
                packs[0, n, g] = low
                packs[1, n, g] = high

        def z_copies(off):
            k = int(off > 0)
            return [remote(packs.at[k], unpacks.at[k], zsend.at[k], zrecv.at[k], 2, off)]

        for off in both:
            start_if(2, off, z_copies(off))
        for off in both:
            recv_if(2, off, z_copies(off))
        for n, ext in enumerate((ue, be)):
            for g in range(groups):
                upper, lower = unpacks[0, n, g], unpacks[1, n, g]
                for k in range(per):
                    up = pltpu.roll(upper, (L - k * H) % L, 1)
                    lo = pltpu.roll(lower, (L - (k + 1) * H) % L, 1)
                    ext[g * per + k, :, L:] = jnp.where(
                        lane < H, up, jnp.where(lane >= L - H, lo, 0.0)
                    )

    def masks_and_diagonals(level, rows, lanes, y_first, y_end, z_of_lane, z_ok, z_first):
        yy = lax.broadcasted_iota(jnp.int32, (rows, lanes), 0)
        zz = lax.broadcasted_iota(jnp.int32, (rows, lanes), 1)
        y_even, z_even = yy % 2 == 0, zz % 2 == 0
        gy = y_first + yy
        gz = z_first + z_of_lane(zz)
        n_y, n_z = (ny * by) >> level, (nz * bz) >> level
        ok = (gy >= 0) & (gy < n_y) & (yy < y_end) & (gz >= 0) & (gz < n_z) & z_ok(zz)
        mask = jnp.where(ok, 1.0, 0.0)
        my = jnp.where(y_even, 8.0, 16.0) / 30.0
        mz = jnp.where(z_even, 8.0, 16.0) / 30.0
        ky = jnp.where(y_even, 14.0, 16.0) / 3.0
        kz = jnp.where(z_even, 14.0, 16.0) / 3.0
        inv = []
        for kx, mx in ((14.0 / 3.0, 8.0 / 30.0), (16.0 / 3.0, 16.0 / 30.0)):
            diag = 2.0**level * (kx * my * mz + mx * ky * mz + mx * my * kz)
            inv.append(mask / diag)
        return mask, inv

    def filter_planes(src, lines, acc, first, pairs):
        rows, lanes = src.shape[1], src.shape[2]

        def body(p, carry):
            x = first + 4 * p
            for k in range(4):
                m, w = z_filters(src[x + k])
                for lt in range(lanes // 128):
                    cut = slice(128 * lt, 128 * lt + 128)
                    lines[k, 0, lt, 8 : 8 + rows] = m[:, cut]
                    lines[k, 1, lt, 8 : 8 + rows] = w[:, cut]
                for lt in range(lanes // 128):
                    for t in range(rows // 16):

                        def rows_of(n, off):
                            return lines[k, n, lt, pl.ds(8 + 16 * t + off, 8, stride=2)]

                        me, mo, we, wo = (
                            rows_of(n, off) for n in range(2) for off in range(2)
                        )
                        next_me, next_we = rows_of(0, 2), rows_of(1, 2)
                        m_e = mo + rows_of(0, -1)
                        w_e = wo + rows_of(1, -1)
                        m_o = me + next_me
                        w_o = we + next_we
                        m_ee = rows_of(0, -2) + next_me
                        w_ee = rows_of(1, -2) + next_we
                        ev = pl.ds(16 * t, 8, stride=2)
                        od = pl.ds(16 * t + 1, 8, stride=2)
                        acc[0, x + k, lt, ev] = 8.0 * me + 2.0 * m_e - m_ee
                        acc[0, x + k, lt, od] = 16.0 * mo + 2.0 * m_o
                        acc[1, x + k, lt, ev] = (22.0 * me - 6.0 * m_e) + (
                            8.0 * we + 2.0 * w_e - w_ee
                        )
                        acc[1, x + k, lt, od] = (32.0 * mo - 6.0 * m_o) + (
                            16.0 * wo + 2.0 * w_o
                        )
            return carry

        lax.fori_loop(0, pl.cdiv(2 * pairs, 4), body, 0)

    def applied(acc, first, pairs, level, use):
        scale = 2.0**level / 2700.0

        def body(p, carry):
            x = first + 2 * p
            for t in range(acc.shape[3] // 8 - 1):
                for lt in range(acc.shape[2]):
                    y = slice(8 * t, 8 * t + 8)
                    a = [acc[0, x + k, lt, y] for k in range(-1, 3)]
                    c = [acc[1, x + k, lt, y] for k in range(-2, 4)]
                    even = (22.0 * a[1] - 6.0 * (a[0] + a[2])) + (
                        8.0 * c[2] + 2.0 * (c[1] + c[3]) - (c[0] + c[4])
                    )
                    odd = (32.0 * a[2] - 6.0 * (a[1] + a[3])) + (
                        16.0 * c[3] + 2.0 * (c[2] + c[4])
                    )
                    use(x, 0, scale * even, t, lt)
                    use(x + 1, 1, scale * odd, t, lt)
            return carry

        lax.fori_loop(0, pairs, body, 0)

    rows0, lanes0 = by + 2 * H, 2 * bz
    mask0, inv0 = masks_and_diagonals(
        0, rows0, lanes0, iy * by - H, rows0,
        lambda z: jnp.where(z < bz + bz // 2, z, z - 2 * bz), lambda z: z >= 0, iz * bz,
    )

    def x_mask(level, x, x_first):
        g = x_first + x
        return jnp.where((g >= 0) & (g < ((nx * bx) >> level)), 1.0, 0.0).astype(F32)

    gx0 = ix * bx - H

    def tile(t, lt):
        return (slice(8 * t, 8 * t + 8), slice(128 * lt, 128 * lt + 128))

    def use_residual(x, odd, av, t, lt):
        y = tile(t, lt)
        r = be[(x, *y)] - av
        r0[(x, *y)] = r
        d0[(x, *y)] = (inv0[odd][y] * (FIRST * x_mask(0, x, gx0))) * r

    filter_planes(ue, y0, a0, 0, (bx + 16) // 2)
    applied(a0, 2, (bx + 12) // 2, 0, use_residual)
    own0 = (slice(H, H + bx), slice(H, H + by), slice(0, bz))
    out_ref[...] = u_ref[...] + d0[own0]

    def use_step(x, odd, av, t, lt):
        y = tile(t, lt)
        r = r0[(x, *y)] - av
        r0[(x, *y)] = r
        d0[(x, *y)] = KEEP * d0[(x, *y)] + (inv0[odd][y] * (STEP * x_mask(0, x, gx0))) * r

    filter_planes(d0, y0, a0, 2, (bx + 12) // 2)
    applied(a0, 4, (bx + 8) // 2, 0, use_step)
    out_ref[...] += d0[own0]

    def use_down(x, odd, av, t, lt):
        y = tile(t, lt)
        r0[(x, *y)] = (r0[(x, *y)] - av) * (mask0[y] * x_mask(0, x, gx0))

    filter_planes(d0, y0, a0, 2, (bx + 10) // 2)
    applied(a0, 4, (bx + 6) // 2, 0, use_down)

    def narrowed(ref, x):
        even = (
            ref[x] + 0.375 * (ref[x - 1] + ref[x + 1]) - 0.125 * (ref[x - 3] + ref[x + 3])
        )
        odd = ref[x + 2] + 0.75 * (ref[x + 1] + ref[x + 3])
        return even, odd

    coarse = []
    for q in range(cx // 2):
        for plane in narrowed(r0, H + 4 * q):
            coarse.append(exact(ry0[...], plane))
    rhs = zdot(jnp.concatenate(coarse, axis=0), rz0[...])
    wl = cz + 2 * ZR
    blk[...] = rhs.reshape(cx, cy, wl)

    if nz > 1:

        def gz_copies(off):
            k = int(off > 0)
            return [remote(blk, zin.at[k], gzsend.at[k], gzrecv.at[k], 2, off)]

        for off in both:
            start_if(2, off, gz_copies(off))
        for off in both:
            recv_if(2, off, gz_copies(off))
        wlane = lax.broadcasted_iota(jnp.int32, (cy, wl), 1)
        for p in range(cx):
            lower = pltpu.roll(zin[1, p], wl - cz, 1)
            upper = pltpu.roll(zin[0, p], cz, 1)
            zin[2, p] = jnp.where(
                wlane < ZR, lower, jnp.where(wlane >= ZR + cz, upper, blk[p])
            )
    else:
        zin[2] = blk[...]

    def slot(axis, off):
        if (full_x, full_y)[axis]:
            return (ix, iy)[axis]
        return REACH - off

    def spot(axis, off, size):
        return pl.ds(pl.multiple_of(slot(axis, off) * size, size), size)

    def gx_copies(off):
        k = off + REACH * 2
        dst = g1.at[spot(0, off, cx), spot(1, 0, cy)]
        return [remote(zin.at[2], dst, gsend.at[0, k], grecv.at[0, k], 0, off)]

    def gy_copies(off):
        k = off + REACH * 2
        src = g1.at[:, spot(1, 0, cy)]
        dst = g1.at[:, spot(1, off, cy)]
        return [remote(src, dst, gsend.at[1, k], grecv.at[1, k], 1, off)]

    for off in offsets[0]:
        start_if(0, off, gx_copies(off))
    g1[spot(0, 0, cx), spot(1, 0, cy)] = zin[2]
    rows1, planes1 = g1.shape[1], cx * wx
    y1[...] = jnp.zeros_like(y1)
    y2[...] = jnp.zeros_like(y2)
    d1[...] = jnp.zeros_like(d1)
    a1[...] = jnp.zeros_like(a1)
    d2[...] = jnp.zeros_like(d2)
    a2[...] = jnp.zeros_like(a2)
    c1[...] = jnp.zeros_like(c1)
    r1[...] = jnp.zeros_like(r1)
    t2[...] = jnp.zeros_like(t2)
    for off in offsets[0]:
        recv_if(0, off, gx_copies(off))
    for off in offsets[1]:
        start_if(1, off, gy_copies(off))
    for off in offsets[1]:
        recv_if(1, off, gy_copies(off))

    Q = 8
    mask1, inv1 = masks_and_diagonals(
        1, rows1, wl, start_y * cy, cy * wy, lambda z: z, lambda z: z >= 0, iz * cz - ZR
    )
    gx1 = start_x * cx - Q

    def first_mid(p, carry):
        for odd in range(2):
            x = 2 * p + odd
            r = g1[x]
            r1[x + Q] = r
            d = (inv1[odd] * (FIRST * x_mask(1, x + Q, gx1))) * r
            d1[x + Q] = d
            s1[x] = d
        return carry

    lax.fori_loop(0, planes1 // 2, first_mid, 0)

    def use_step1(x, odd, av, t, lt):
        y = tile(t, lt)
        r = r1[(x, *y)] - av
        r1[(x, *y)] = r
        d = KEEP * d1[(x, *y)] + (inv1[odd][y] * (STEP * x_mask(1, x, gx1))) * r
        d1[(x, *y)] = d
        s1[(x - Q, *y)] += d

    def use_down1(x, odd, av, t, lt):
        y = tile(t, lt)
        r1[(x, *y)] = (r1[(x, *y)] - av) * (mask1[y] * x_mask(1, x, gx1))

    half1 = planes1 // 2
    filter_planes(d1, y1, a1, Q, half1)
    applied(a1, Q, half1, 1, use_step1)
    filter_planes(d1, y1, a1, Q, half1)
    applied(a1, Q, half1, 1, use_down1)

    planes2 = planes1 // 2
    rows2 = d2.shape[1]
    mask2, inv2 = masks_and_diagonals(
        2, rows2, wl, start_y * (cy // 2), cy * wy // 2, lambda z: z,
        lambda z: z < wl // 2, iz * (cz // 2) - ZR // 2,
    )
    gx2 = start_x * (cx // 2) - Q

    def down_mid(q, carry):
        parts = [exact(ry1[...], plane) for plane in narrowed(r1, Q + 4 * q)]
        prod = zdot(jnp.concatenate(parts, axis=0), rz1[...])
        for odd in range(2):
            x = 2 * q + odd + Q
            r = prod[odd * rows2 : (odd + 1) * rows2]
            r2[x] = r
            d2[x] = (inv2[odd] * (FIRST * x_mask(2, x, gx2))) * r
        return carry

    lax.fori_loop(0, planes2 // 2, down_mid, 0)
    filter_planes(d2, y2, a2, Q, planes2 // 2)

    def use_last(x, odd, av, t, lt):
        y = tile(t, lt)
        r = r2[(x, *y)] - av
        step = (inv2[odd][y] * (STEP * x_mask(2, x, gx2))) * r
        d2[(x, *y)] = (1.0 + KEEP) * d2[(x, *y)] + step

    applied(a2, Q, planes2 // 2, 2, use_last)

    def up_last(p, carry):
        v = zdot(d2[pl.ds(Q + 2 * p, 2)].reshape(2 * rows2, wl), pz1[...])
        for k in range(2):
            t2[2 * p + k] = exact(py1[...], v[k * rows2 : (k + 1) * rows2])
        return carry

    lax.fori_loop(0, planes2 // 2, up_last, 0)

    def widened(ref, x):
        one, two, three = ref[x], ref[x + 1], ref[x + 2]
        return (
            one,
            0.375 * one + 0.75 * two - 0.125 * three,
            two,
            -0.125 * one + 0.75 * two + 0.375 * three,
        )

    def up_mid(q, carry):
        for k, plane in enumerate(widened(t2, 2 * q)):
            x = 4 * q + k
            e = plane * (mask1 * x_mask(1, x + Q, gx1))
            d1[x + Q] = e
            s1[x] += e
        return carry

    lax.fori_loop(0, planes1 // 4, up_mid, 0)
    filter_planes(d1, y1, a1, Q, half1)

    def use_up1(x, odd, av, t, lt):
        y = tile(t, lt)
        r = r1[(x, *y)] - av
        r1[(x, *y)] = r
        d = (inv1[odd][y] * (FIRST * x_mask(1, x, gx1))) * r
        d1[(x, *y)] = d
        s1[(x - Q, *y)] += d

    applied(a1, Q, half1, 1, use_up1)
    filter_planes(d1, y1, a1, Q, half1)

    def use_final1(x, odd, av, t, lt):
        y = tile(t, lt)
        r = r1[(x, *y)] - av
        d = KEEP * d1[(x, *y)] + (inv1[odd][y] * (STEP * x_mask(1, x, gx1))) * r
        c1[(x, *tile(t + 1, lt))] = s1[(x - Q, *y)] + d

    applied(a1, Q, half1, 1, use_final1)

    crow = cy + 16
    own_x = (ix if full_x else REACH) * cx + Q
    own_y = pl.multiple_of((iy if full_y else REACH) * cy, 8)

    def up_first(p, carry):
        x = own_x - 2 + 2 * p
        v = c1[pl.ds(x, 2), pl.ds(own_y, crow)].reshape(2 * crow, wl)
        v = zdot(v, pz0[...])
        for k in range(2):
            c0[2 * p + k] = exact(py0[...], v[k * crow : (k + 1) * crow])
        return carry

    lax.fori_loop(0, (cx + 6) // 2, up_first, 0)

    def up_fine(q, carry):
        for k, plane in enumerate(widened(c0, 2 * q)):
            x = H - 4 + 4 * q + k
            d0[x] = plane * (mask0 * x_mask(0, x, gx0))
        return carry

    lax.fori_loop(0, (bx + 8) // 4, up_fine, 0)
    out_ref[...] += d0[own0]
    filter_planes(d0, y0, a0, 4, (bx + 8) // 2)

    def use_up(x, odd, av, t, lt):
        y = tile(t, lt)
        r = r0[(x, *y)] - av
        r0[(x, *y)] = r
        d0[(x, *y)] = (inv0[odd][y] * (FIRST * x_mask(0, x, gx0))) * r

    applied(a0, 6, (bx + 4) // 2, 0, use_up)
    filter_planes(d0, y0, a0, 6, (bx + 4) // 2)

    def use_final(x, odd, av, t, lt):
        if t == 0 or t == by // 8 + 1 or lt >= bz // 128:
            return
        y = tile(t, lt)
        r = r0[(x, *y)] - av
        d = d0[(x, *y)]
        new = d + (KEEP * d + (inv0[odd][y] * STEP) * r)
        out_ref[(x - H, *tile(t - 1, lt))] += new

    applied(a0, H, bx // 2, 0, use_final)

    for off in both:
        sent_if(0, off, x_copies(off))
        sent_if(1, off, y_copies(off) + corner_copies(off))
        if nz > 1:
            sent_if(2, off, z_copies(off) + gz_copies(off))
    for off in offsets[0]:
        sent_if(0, off, gx_copies(off))
    for off in offsets[1]:
        sent_if(1, off, gy_copies(off))


def local(mesh_shape, u, b):
    nx, ny, nz = (mesh_shape[a] for a in ("gx", "gy", "gz"))
    bx, by, bz = u.shape
    cx, cy, cz = bx // 2, by // 2, bz // 2
    wx = nx if nx <= 2 * REACH + 1 else 2 * REACH + 1
    wy = ny if ny <= 2 * REACH + 1 else 2 * REACH + 1
    wl = cz + 2 * ZR
    rows0, lanes0 = by + 2 * H, 2 * bz
    rows1, planes1 = -(-cy * wy // 16) * 16, cx * wx
    rows2, planes2 = -(-cy * wy // 32) * 16, planes1 // 2
    crow = cy + 16

    def z_pos(z):
        return z if z >= 0 else z + lanes0

    rz0 = transfer(restrict_taps, range(cz), lambda o: o + ZR, z_pos, wl, lanes0, 2).T
    ry0 = transfer(restrict_taps, range(cy), lambda o: o, lambda f: f + H, cy, rows0, 2)
    rz1 = transfer(restrict_taps, range(wl // 2), lambda o: o, lambda f: f, wl, wl, 2).T
    live1 = lambda f: f if 0 <= f < cy * wy else None
    ry1 = transfer(restrict_taps, range(cy * wy // 2), lambda o: o, live1, rows2, rows1, 2)
    pz1 = transfer(prolong_taps, range(wl), lambda o: o, lambda c: c, wl, wl, 0).T
    live2 = lambda c: c if 0 <= c < cy * wy // 2 else None
    py1 = transfer(prolong_taps, range(cy * wy), lambda o: o, live2, rows1, rows2, 0)
    pz0 = transfer(
        prolong_taps, range(-H, bz + H), z_pos, lambda c: c + ZR, lanes0, wl, 0
    ).T
    py0 = transfer(
        prolong_taps, range(-H, by + H), lambda o: o + H, lambda c: c + 8, rows0, crow, 0
    )
    bf = lambda m: jnp.asarray(m, BF16)
    fl = lambda m: jnp.asarray(m, F32)
    consts = (
        bf(rz0), fl(ry0), bf(rz1), fl(ry1), bf(pz1), fl(py1),
        bf(pz0), fl(py0),
    )
    vm = lambda *s: pltpu.VMEM(s, F32)
    groups = (bx + 2 * H) // (bz // H)
    dma = lambda *s: pltpu.SemaphoreType.DMA(s)
    geo = (nx, ny, nz, bx, by, bz, wx, wy)
    return pl.pallas_call(
        functools.partial(kernel, geo),
        out_shape=jax.ShapeDtypeStruct(u.shape, F32),
        in_specs=[pl.BlockSpec(memory_space=pltpu.VMEM)] * (2 + len(consts)),
        out_specs=pl.BlockSpec(memory_space=pltpu.VMEM),
        scratch_shapes=[
            vm(bx + 16, rows0, lanes0), vm(bx + 16, rows0, lanes0),
            vm(bx + 16, rows0, lanes0), vm(bx + 16, rows0, lanes0),
            vm(2, bx + 16, lanes0 // 128, rows0 + 8, 128), vm(cx + 8, rows0, lanes0),
            vm(2, 2, groups, rows0, bz), vm(2, 2, groups, rows0, bz),
            vm(4, 2, lanes0 // 128, rows0 + 16, 128), vm(4, 2, wl // 128, rows1 + 16, 128),
            vm(4, 2, wl // 128, rows2 + 16, 128), vm(cx, cy, wl), vm(3, cx, cy, wl),
            vm(planes1, rows1, wl), vm(planes1 + 16, rows1, wl),
            vm(planes1 + 16, rows1, wl), vm(planes1, rows1, wl),
            vm(2, planes1 + 16, wl // 128, rows1 + 8, 128), vm(planes1 + 16, rows1 + 16, wl),
            vm(planes2 + 16, rows2, wl), vm(planes2 + 16, rows2, wl),
            vm(2, planes2 + 16, wl // 128, rows2 + 8, 128), vm(planes2 + 8, rows1, wl),
            dma(16), dma(16), dma(2), dma(2),
            dma(2, 4 * REACH + 1), dma(2, 4 * REACH + 1), dma(2), dma(2),
        ],
        compiler_params=pltpu.CompilerParams(
            collective_id=0, has_side_effects=True, vmem_limit_bytes=60 * 1024 * 1024
        ),
    )(u, b, *consts)


def solution(mesh):
    placed = P("gx", "gy", "gz")
    return jax.shard_map(
        functools.partial(local, dict(mesh.shape)), mesh=mesh,
        in_specs=(placed, placed), out_specs=placed, check_vma=False,
    )
```
